256 devices in a mesh: section: 4 (over y), tm: 64 (over z, x, core).
Axes of the slice: x: 4, y: 4, z: 8, core: 2. Of those that a mesh axis runs over, the one named last changes fastest.
Arguments:
- inputs: bfloat16 [3, 8192, 1024], P(None, 'tm', 'section'), may hold values from -6 to 6
- lengths: int32 [3], replicated, may hold values from 2048 to 8192, as said below
- w_expand: bfloat16 [2, 4, 1024, 2048], P(None, 'section'), may hold values from -0.1875 to 0.1875
- w_project: bfloat16 [2, 4, 1024, 1024], P(None, 'section'), may hold values from -0.1875 to 0.1875
- kernel: float32 [2, 4, 32, 1024], P(None, 'section'), may hold values from -1.5 to 1.5
- gain: float32 [2, 4, 1024], P(None, 'section'), may hold values from 0.1 to 1.9
Outputs:
- encoded: bfloat16 [3, 8192, 1024], P(None, 'tm', 'section')
The draws below stay inside these ranges and needn't reach their ends.
Inputs may be any that keep to these rules, and one draw needn't show every extreme that they name: lengths[0] is 8192.
All inputs are finite; a program needn't handle non-finite values.
Results may differ from the reference program's by a relative error of at most 0.022.
Values may be sent and summed in bfloat16 or wider, within the bound.
A program may use at most 64 MiB of HBM per device.

```python
import jax
import jax.numpy as jnp
from jax import lax

D = 1024
KW = 32
PASSES = 2
MB = 3
FRAMES = 8192
N_SECTION = 4


def draw_lengths(key, part):
    values = jax.random.randint(key, (MB,), FRAMES // 4, FRAMES + 1)
    return jnp.where(jnp.arange(MB) == 0, FRAMES, values).astype(jnp.int32)


def shard_levels(own_key, dims, cuts, least, high):
    level = 1.0
    for dim, blocks in cuts:
        heights = jax.random.uniform(jax.random.fold_in(jax.random.fold_in(own_key, 6), dim), (blocks,), jnp.float32, least / len(cuts), high / len(cuts))
        level = level * jnp.repeat(jnp.exp(heights), dims[dim] // blocks).reshape((-1,) + (1,) * (len(dims) - 1 - dim))
    return level


def scatter_about(own_key, extent, spread, reach, pieces=(), held_as=jnp.bfloat16):
    array = spread * jax.random.normal(own_key, extent, jnp.float32)
    if pieces:
        array = array * shard_levels(own_key, extent, pieces, -0.22, 0.18)
    return jnp.clip(array, -reach, reach).astype(held_as)


def setup_inputs(seed: int = 0) -> dict:
    splits = jax.random.split(jax.random.key(seed), 7)
    return {
        "inputs": scatter_about(splits[0], (MB, FRAMES, D), 1.0, 6.0, ((1, 64), (2, 4))),
        "lengths": draw_lengths(jax.random.fold_in(splits[6], 71), 0),
        "w_expand": scatter_about(splits[2], (PASSES, N_SECTION, D, 2 * D), D ** -0.5, 0.1875, ((1, 4),)),
        "w_project": scatter_about(splits[3], (PASSES, N_SECTION, D, D), D ** -0.5, 0.1875, ((1, 4),)),
        "kernel": scatter_about(splits[4], (PASSES, N_SECTION, KW, D), (KW // 2) ** -0.5, 1.5, ((1, 4),), jnp.float32),
        "gain": jnp.clip(1.0 + 0.18 * jax.random.normal(splits[5], (PASSES, N_SECTION, D), jnp.float32), 0.1, 1.9),
    }


def layer_norm(values):
    center = values - lax.optimization_barrier(jnp.mean(values, axis=-1, keepdims=True))
    variance = lax.optimization_barrier(jnp.mean(center * center, axis=-1, keepdims=True))
    return center * lax.rsqrt(variance + 1e-05)

def conv_layer(stream, frame_mask, w_first, w_second, taps, scale):
    feats = stream.shape[1]
    normed = (layer_norm(stream.astype(jnp.float32)) * scale).astype(jnp.bfloat16)
    expanded = jnp.dot(normed, w_first, preferred_element_type=jnp.float32)
    gated = (expanded[:, :feats] * jax.nn.sigmoid(expanded[:, feats:]) * frame_mask[:, None]).astype(jnp.bfloat16)
    width = taps.shape[0]
    padded = jnp.concatenate([jnp.zeros((width - 1, feats), jnp.bfloat16), gated], axis=0)
    count = stream.shape[0]
    depthwise = jnp.zeros((count, feats), jnp.float32)
    for offset in range(width):
        depthwise = depthwise + taps[offset][None, :] * padded[offset:offset + count].astype(jnp.float32)
    activated = jax.nn.silu(layer_norm(depthwise)).astype(jnp.bfloat16)
    summed = stream.astype(jnp.float32) + jnp.dot(activated, w_second, preferred_element_type=jnp.float32)
    return (summed * frame_mask[:, None]).astype(jnp.bfloat16)

def reference(inputs, lengths, w_expand, w_project, kernel, gain):
    positions = jnp.arange(FRAMES, dtype=jnp.int32)
    results = []
    for micro in range(MB):
        frame_mask = (positions < lengths[micro]).astype(jnp.float32)
        stream = inputs[micro]
        for pass_idx in range(PASSES):
            for section_idx in range(N_SECTION):
                stream = conv_layer(stream, frame_mask, w_expand[pass_idx, section_idx], w_project[pass_idx, section_idx], kernel[pass_idx, section_idx], gain[pass_idx, section_idx])
        results.append(stream)
    return jnp.stack(results, axis=0)
```

```python
import functools

import jax
import jax.numpy as jnp
from jax import lax
from jax.experimental import pallas as pl
from jax.experimental.pallas import tpu as pltpu
from jax.sharding import PartitionSpec as P

MESH = pl.DeviceIdType.MESH
ROWS = 32
HALO = 32
COLS = 256


def normalise(values):
    center = values - jnp.mean(values, axis=-1, keepdims=True)
    variance = jnp.mean(center * center, axis=-1, keepdims=True)
    return center * lax.rsqrt(variance + 1e-05)


def relay_kernel(
    sections,
    tms,
    lengths_ref,
    inputs_hbm,
    w_expand_hbm,
    w_project_hbm,
    kernel_hbm,
    gain_hbm,
    out_hbm,
    w1,
    w2,
    taps,
    gain,
    wide_taps,
    slots,
    outs,
    rims,
    tails,
    gated,
    depthwise,
    w_sems,
    small_sems,
    slot_send,
    slot_recv,
    rim_send,
    rim_recv,
    entry_send,
    entry_recv,
    exit_send,
    exit_recv,
):
    section = lax.axis_index("section")
    tm = lax.axis_index("tm")
    micro, frames, width = inputs_hbm.shape
    passes, feats, _ = w1.shape
    taps_len = taps.shape[1]
    chunks = frames // ROWS
    jobs = micro * passes
    last = sections - 1

    def weight_copies(pass_idx):
        return (
            pltpu.make_async_copy(w_expand_hbm.at[pass_idx], w1.at[pass_idx], w_sems.at[0, pass_idx]),
            pltpu.make_async_copy(w_project_hbm.at[pass_idx], w2.at[pass_idx], w_sems.at[1, pass_idx]),
        )

    taps_copy = pltpu.make_async_copy(kernel_hbm, taps, small_sems.at[0])
    gain_copy = pltpu.make_async_copy(gain_hbm, gain, small_sems.at[1])
    taps_copy.start()
    gain_copy.start()
    for copy in weight_copies(0):
        copy.start()
    for copy in weight_copies(1):
        copy.start()

    barrier = pltpu.get_barrier_semaphore()
    for step in range(1, sections):
        pl.semaphore_signal(
            barrier, inc=1, device_id={"section": (section + step) % sections}, device_id_type=MESH
        )

    @pl.when(tm > 0)
    def _():
        pl.semaphore_signal(barrier, inc=1, device_id={"tm": tm - 1}, device_id_type=MESH)

    @pl.when(tm < tms - 1)
    def _():
        pl.semaphore_signal(barrier, inc=1, device_id={"tm": tm + 1}, device_id_type=MESH)

    greeted = sections - 1 + (tm > 0).astype(jnp.int32) + (tm < tms - 1).astype(jnp.int32)
    pl.semaphore_wait(barrier, greeted)

    def entry_remote(m, source):
        return pltpu.make_async_remote_copy(
            src_ref=inputs_hbm.at[m],
            dst_ref=slots.at[m, :, pl.ds(pl.multiple_of(source * width, width), width)],
            send_sem=entry_send.at[m],
            recv_sem=entry_recv.at[m, source],
            device_id={"section": 0},
            device_id_type=MESH,
        )

    def entry_local(m):
        return pltpu.make_async_copy(
            inputs_hbm.at[m], slots.at[m, :, pl.ds(0, width)], entry_recv.at[m, 0]
        )

    @pl.when(section == 0)
    def _():
        for m in range(micro):
            entry_local(m).start()

    @pl.when(section != 0)
    def _():
        for m in range(micro):
            entry_remote(m, section).start()

    taps_copy.wait()
    gain_copy.wait()
    for pass_idx in range(passes):
        for k in range(taps_len):
            wide_taps[pass_idx, k] = jnp.broadcast_to(taps[pass_idx, k : k + 1, :], (8, feats))

    def slot_copy(job, chunk):
        slot = job + jnp.where(section == last, micro, 0)
        rows = pl.ds(pl.multiple_of(chunk * ROWS, ROWS), ROWS)
        return pltpu.make_async_remote_copy(
            src_ref=outs.at[job, rows],
            dst_ref=slots.at[slot, rows],
            send_sem=slot_send.at[job, chunk],
            recv_sem=slot_recv.at[slot, chunk],
            device_id={"section": (section + 1) % sections},
            device_id_type=MESH,
        )

    def slot_arrival(job, chunk):
        rows = pl.ds(pl.multiple_of(chunk * ROWS, ROWS), ROWS)
        return pltpu.make_async_remote_copy(
            src_ref=outs.at[job, rows],
            dst_ref=slots.at[job, rows],
            send_sem=slot_send.at[job, chunk],
            recv_sem=slot_recv.at[job, chunk],
            device_id={"section": (section + 1) % sections},
            device_id_type=MESH,
        )

    def rim_copy(job):
        return pltpu.make_async_remote_copy(
            src_ref=tails.at[job],
            dst_ref=rims.at[job],
            send_sem=rim_send.at[job],
            recv_sem=rim_recv.at[job],
            device_id={"tm": tm + 1},
            device_id_type=MESH,
        )

    def exit_remote(m, chunk, target):
        rows = pl.ds(pl.multiple_of(chunk * ROWS, ROWS), ROWS)
        return pltpu.make_async_remote_copy(
            src_ref=outs.at[m + (jobs - micro), rows, pl.ds(target * width, width)],
            dst_ref=out_hbm.at[m, rows],
            send_sem=exit_send.at[m, chunk, target],
            recv_sem=exit_recv.at[m, chunk],
            device_id={"section": target},
            device_id_type=MESH,
        )

    def exit_local(m, chunk):
        rows = pl.ds(pl.multiple_of(chunk * ROWS, ROWS), ROWS)
        return pltpu.make_async_copy(
            outs.at[m + (jobs - micro), rows, pl.ds(last * width, width)],
            out_hbm.at[m, rows],
            exit_recv.at[m, chunk],
        )

    def run_job(job, _):
        pass_idx = job // micro
        m = job % micro
        length = lengths_ref[m]
        first = jnp.logical_and(section == 0, pass_idx == 0)
        leaving = jnp.logical_and(section == last, pass_idx == passes - 1)

        def row_mask(chunk):
            rows = lax.broadcasted_iota(jnp.int32, (ROWS, 1), 0) + (tm * frames + chunk * ROWS)
            return rows < length

        @pl.when(first)
        def _():
            entry_local(m).wait()
            for source in range(1, sections):
                entry_remote(m, source).wait_recv()

        def expand(chunk):
            @pl.when(jnp.logical_not(first))
            def _():
                slot_arrival(job, chunk).wait_recv()

            if chunk == chunks - 1:

                @pl.when(m == 0)
                def _():
                    weight_copies(pass_idx)[0].wait()

            values = slots[job, chunk * ROWS : (chunk + 1) * ROWS, :].astype(jnp.float32)
            normed = (normalise(values) * gain[pass_idx]).astype(jnp.bfloat16)
            mask = row_mask(chunk)
            for block in range(feats // COLS):
                low = block * COLS
                value = jnp.dot(
                    normed, w1[pass_idx, :, low : low + COLS], preferred_element_type=jnp.float32
                )
                gate = jnp.dot(
                    normed,
                    w1[pass_idx, :, feats + low : feats + low + COLS],
                    preferred_element_type=jnp.float32,
                )
                passed = jnp.where(mask, value * jax.nn.sigmoid(gate), 0.0).astype(jnp.bfloat16)
                gated[HALO + chunk * ROWS : HALO + (chunk + 1) * ROWS, low : low + COLS] = (
                    passed.astype(jnp.float32)
                )
                if chunk == chunks - 1:
                    tails[job, :, low : low + COLS] = passed[ROWS - HALO :, :]
            if chunk == chunks - 1:

                @pl.when(tm < tms - 1)
                def _():
                    rim_copy(job).start()

        def finish(chunk):
            for block in range(feats // 128):
                cols = slice(block * 128, (block + 1) * 128)
                window = gated[chunk * ROWS : (chunk + 1) * ROWS + HALO, cols]
                total = jnp.zeros((ROWS // 8, 8, 128), jnp.float32)
                for back in range(8):
                    moved = window if back == 0 else pltpu.roll(window, back, 0)
                    tiles = moved.reshape((ROWS + HALO) // 8, 8, 128)
                    for group in range(taps_len // 8):
                        tap = wide_taps[pass_idx, taps_len - 1 - 8 * group - back, :, cols]
                        start = HALO // 8 - group
                        total = total + tap[None] * tiles[start : start + ROWS // 8]
                depthwise[:, cols] = total.reshape(ROWS, 128)
            hidden = normalise(depthwise[...])
            activated = (hidden * jax.nn.sigmoid(hidden)).astype(jnp.bfloat16)
            mask = row_mask(chunk)
            if chunk == chunks - 1:

                @pl.when(m == 0)
                def _():
                    weight_copies(pass_idx)[1].wait()

            rows = slice(chunk * ROWS, (chunk + 1) * ROWS)
            for block in range(feats // COLS):
                cols = slice(block * COLS, (block + 1) * COLS)
                added = slots[job, rows, cols].astype(jnp.float32) + jnp.dot(
                    activated, w2[pass_idx, :, cols], preferred_element_type=jnp.float32
                )
                outs[job, rows, cols] = jnp.where(mask, added, 0.0).astype(jnp.bfloat16)

            @pl.when(leaving)
            def _():
                for target in range(last):
                    exit_remote(m, chunk, target).start()
                exit_local(m, chunk).start()

            @pl.when(jnp.logical_not(leaving))
            def _():
                slot_copy(job, chunk).start()

        for chunk in reversed(range(chunks)):
            expand(chunk)
            if chunk < chunks - 1:
                finish(chunk + 1)

        @pl.when(tm > 0)
        def _():
            rim_copy(job).wait_recv()
            gated[0:HALO, :] = rims[job].astype(jnp.float32)

        @pl.when(tm == 0)
        def _():
            gated[0:HALO, :] = jnp.zeros((HALO, feats), jnp.float32)

        finish(0)
        return 0

    lax.fori_loop(0, jobs, run_job, 0)

    @pl.when(section != 0)
    def _():
        for m in range(micro):
            entry_remote(m, section).wait_send()

    def drain(job, _):
        leaving = jnp.logical_and(section == last, job >= jobs - micro)

        @pl.when(tm < tms - 1)
        def _():
            rim_copy(job).wait_send()

        for chunk in range(chunks):

            @pl.when(jnp.logical_not(leaving))
            def _():
                slot_copy(job, chunk).wait_send()

        return 0

    lax.fori_loop(0, jobs, drain, 0)

    @pl.when(section == last)
    def _():
        for m in range(micro):
            for chunk in range(chunks):
                for target in range(last):
                    exit_remote(m, chunk, target).wait_send()
                exit_local(m, chunk).wait()

    @pl.when(section != last)
    def _():
        for m in range(micro):
            for chunk in range(chunks):
                exit_remote(m, chunk, 0).wait_recv()


def per_device(inputs, lengths, w_expand, w_project, kernel, gain):
    sections = lax.axis_size("section")
    tms = lax.axis_size("tm")
    micro, frames, width = inputs.shape
    passes, _, feats, expanded = w_expand.shape
    taps = kernel.shape[2]
    chunks = frames // ROWS
    jobs = micro * passes
    hbm = pl.BlockSpec(memory_space=pl.ANY)
    dma = pltpu.SemaphoreType.DMA
    return pl.pallas_call(
        functools.partial(relay_kernel, sections, tms),
        out_shape=jax.ShapeDtypeStruct((micro, frames, width), jnp.bfloat16),
        in_specs=[pl.BlockSpec(memory_space=pltpu.SMEM)] + [hbm] * 5,
        out_specs=hbm,
        scratch_shapes=[
            pltpu.VMEM((passes, feats, expanded), jnp.bfloat16),
            pltpu.VMEM((passes, feats, feats), jnp.bfloat16),
            pltpu.VMEM((passes, taps, feats), jnp.float32),
            pltpu.VMEM((passes, 1, feats), jnp.float32),
            pltpu.VMEM((passes, taps, 8, feats), jnp.float32),
            pltpu.VMEM((jobs, frames, feats), jnp.bfloat16),
            pltpu.VMEM((jobs, frames, feats), jnp.bfloat16),
            pltpu.VMEM((jobs, HALO, feats), jnp.bfloat16),
            pltpu.VMEM((jobs, HALO, feats), jnp.bfloat16),
            pltpu.VMEM((HALO + frames, feats), jnp.float32),
            pltpu.VMEM((ROWS, feats), jnp.float32),
            dma((2, passes)),
            dma((2,)),
            dma((jobs, chunks)),
            dma((jobs, chunks)),
            dma((jobs,)),
            dma((jobs,)),
            dma((micro,)),
            dma((micro, sections)),
            dma((micro, chunks, sections)),
            dma((micro, chunks)),
        ],
        compiler_params=pltpu.CompilerParams(
            collective_id=0, has_side_effects=True, vmem_limit_bytes=40 << 20
        ),
        name="relay",
    )(
        lengths,
        inputs,
        w_expand.reshape(passes, feats, expanded),
        w_project.reshape(passes, feats, feats),
        kernel.reshape(passes, taps, feats),
        gain,
    )


def solution(mesh):
    in_specs = (
        P(None, "tm", "section"),
        P(),
        P(None, "section", None, None),
        P(None, "section", None, None),
        P(None, "section", None, None),
        P(None, "section", None),
    )
    out_specs = P(None, "tm", "section")
    return jax.shard_map(
        per_device, mesh=mesh, in_specs=in_specs, out_specs=out_specs, check_vma=False
    )
```

```python
import functools

import jax
import jax.numpy as jnp
from jax import lax
from jax.experimental import pallas as pl
from jax.experimental.pallas import tpu as pltpu
from jax.sharding import PartitionSpec as P

MESH = pl.DeviceIdType.MESH
ROWS = 32
HALO = 32
COLS = 256


def normalise(values):
    center = values - jnp.mean(values, axis=-1, keepdims=True)
    variance = jnp.mean(center * center, axis=-1, keepdims=True)
    return center * lax.rsqrt(variance + 1e-05)


def relay_kernel(
    sections,
    tms,
    lengths_ref,
    inputs_hbm,
    w_expand_hbm,
    w_project_hbm,
    kernel_hbm,
    gain_hbm,
    out_hbm,
    w1,
    w2,
    taps,
    gain,
    wide_taps,
    slots,
    outs,
    rims,
    tails,
    gated,
    depthwise,
    w_sems,
    small_sems,
    slot_send,
    slot_recv,
    rim_send,
    rim_recv,
    entry_send,
    entry_recv,
    exit_send,
    exit_recv,
):
    section = lax.axis_index("section")
    tm = lax.axis_index("tm")
    micro, frames, width = inputs_hbm.shape
    passes, feats, _ = w1.shape
    taps_len = taps.shape[1]
    chunks = frames // ROWS
    jobs = micro * passes
    last = sections - 1

    def weight_copies(pass_idx):
        return (
            pltpu.make_async_copy(w_expand_hbm.at[pass_idx], w1.at[pass_idx], w_sems.at[0, pass_idx]),
            pltpu.make_async_copy(w_project_hbm.at[pass_idx], w2.at[pass_idx], w_sems.at[1, pass_idx]),
        )

    taps_copy = pltpu.make_async_copy(kernel_hbm, taps, small_sems.at[0])
    gain_copy = pltpu.make_async_copy(gain_hbm, gain, small_sems.at[1])
    taps_copy.start()
    gain_copy.start()
    for copy in weight_copies(0):
        copy.start()
    for copy in weight_copies(1):
        copy.start()

    barrier = pltpu.get_barrier_semaphore()
    for step in range(1, sections):
        pl.semaphore_signal(
            barrier, inc=1, device_id={"section": (section + step) % sections}, device_id_type=MESH
        )

    @pl.when(tm > 0)
    def _():
        pl.semaphore_signal(barrier, inc=1, device_id={"tm": tm - 1}, device_id_type=MESH)

    @pl.when(tm < tms - 1)
    def _():
        pl.semaphore_signal(barrier, inc=1, device_id={"tm": tm + 1}, device_id_type=MESH)

    greeted = sections - 1 + (tm > 0).astype(jnp.int32) + (tm < tms - 1).astype(jnp.int32)
    pl.semaphore_wait(barrier, greeted)

    def entry_remote(m, chunk, source):
        rows = pl.ds(chunk * ROWS, ROWS)
        return pltpu.make_async_remote_copy(
            src_ref=inputs_hbm.at[m, rows],
            dst_ref=slots.at[m, rows, pl.ds(pl.multiple_of(source * width, width), width)],
            send_sem=entry_send.at[m, chunk],
            recv_sem=entry_recv.at[m, chunk, source],
            device_id={"section": 0},
            device_id_type=MESH,
        )

    def entry_local(m, chunk):
        rows = pl.ds(chunk * ROWS, ROWS)
        return pltpu.make_async_copy(
            inputs_hbm.at[m, rows], slots.at[m, rows, pl.ds(0, width)], entry_recv.at[m, chunk, 0]
        )

    @pl.when(section == 0)
    def _():
        for m in range(micro):
            for chunk in reversed(range(chunks)):
                entry_local(m, chunk).start()

    @pl.when(section != 0)
    def _():
        for m in range(micro):
            for chunk in reversed(range(chunks)):
                entry_remote(m, chunk, section).start()
            for chunk in reversed(range(chunks)):
                entry_remote(m, chunk, section).wait_send()

    taps_copy.wait()
    gain_copy.wait()
    for pass_idx in range(passes):
        for k in range(taps_len):
            wide_taps[pass_idx, k] = jnp.broadcast_to(taps[pass_idx, k : k + 1, :], (8, feats))

    def slot_copy(job, chunk):
        slot = job + jnp.where(section == last, micro, 0)
        rows = pl.ds(pl.multiple_of(chunk * ROWS, ROWS), ROWS)
        return pltpu.make_async_remote_copy(
            src_ref=outs.at[job, rows],
            dst_ref=slots.at[slot, rows],
            send_sem=slot_send.at[job, chunk],
            recv_sem=slot_recv.at[slot, chunk],
            device_id={"section": (section + 1) % sections},
            device_id_type=MESH,
        )

    def slot_arrival(job, chunk):
        rows = pl.ds(pl.multiple_of(chunk * ROWS, ROWS), ROWS)
        return pltpu.make_async_remote_copy(
            src_ref=outs.at[job, rows],
            dst_ref=slots.at[job, rows],
            send_sem=slot_send.at[job, chunk],
            recv_sem=slot_recv.at[job, chunk],
            device_id={"section": (section + 1) % sections},
            device_id_type=MESH,
        )

    def rim_copy(job):
        return pltpu.make_async_remote_copy(
            src_ref=tails.at[job],
            dst_ref=rims.at[job],
            send_sem=rim_send.at[job],
            recv_sem=rim_recv.at[job],
            device_id={"tm": tm + 1},
            device_id_type=MESH,
        )

    def exit_remote(m, chunk, target):
        rows = pl.ds(pl.multiple_of(chunk * ROWS, ROWS), ROWS)
        return pltpu.make_async_remote_copy(
            src_ref=outs.at[m + (jobs - micro), rows, pl.ds(target * width, width)],
            dst_ref=out_hbm.at[m, rows],
            send_sem=exit_send.at[m, chunk, target],
            recv_sem=exit_recv.at[m, chunk],
            device_id={"section": target},
            device_id_type=MESH,
        )

    def exit_local(m, chunk):
        rows = pl.ds(pl.multiple_of(chunk * ROWS, ROWS), ROWS)
        return pltpu.make_async_copy(
            outs.at[m + (jobs - micro), rows, pl.ds(last * width, width)],
            out_hbm.at[m, rows],
            exit_recv.at[m, chunk],
        )

    def run_job(job, _):
        pass_idx = job // micro
        m = job % micro
        length = lengths_ref[m]
        first = jnp.logical_and(section == 0, pass_idx == 0)
        leaving = jnp.logical_and(section == last, pass_idx == passes - 1)

        def row_mask(chunk):
            rows = lax.broadcasted_iota(jnp.int32, (ROWS, 1), 0) + (tm * frames + chunk * ROWS)
            return rows < length

        def expand(chunk):
            @pl.when(first)
            def _():
                entry_local(m, chunk).wait()
                for source in range(1, sections):
                    entry_remote(m, chunk, source).wait_recv()

            @pl.when(jnp.logical_not(first))
            def _():
                slot_arrival(job, chunk).wait_recv()

            if chunk == chunks - 1:

                @pl.when(m == 0)
                def _():
                    weight_copies(pass_idx)[0].wait()

            values = slots[job, chunk * ROWS : (chunk + 1) * ROWS, :].astype(jnp.float32)
            normed = (normalise(values) * gain[pass_idx]).astype(jnp.bfloat16)
            mask = row_mask(chunk)
            for block in range(feats // COLS):
                low = block * COLS
                value = jnp.dot(
                    normed, w1[pass_idx, :, low : low + COLS], preferred_element_type=jnp.float32
                )
                gate = jnp.dot(
                    normed,
                    w1[pass_idx, :, feats + low : feats + low + COLS],
                    preferred_element_type=jnp.float32,
                )
                passed = jnp.where(mask, value * jax.nn.sigmoid(gate), 0.0).astype(jnp.bfloat16)
                gated[HALO + chunk * ROWS : HALO + (chunk + 1) * ROWS, low : low + COLS] = (
                    passed.astype(jnp.float32)
                )
                if chunk == chunks - 1:
                    tails[job, :, low : low + COLS] = passed[ROWS - HALO :, :]
            if chunk == chunks - 1:

                @pl.when(tm < tms - 1)
                def _():
                    rim_copy(job).start()

        def finish(chunk):
            for block in range(feats // 128):
                cols = slice(block * 128, (block + 1) * 128)
                window = gated[chunk * ROWS : (chunk + 1) * ROWS + HALO, cols]
                total = jnp.zeros((ROWS // 8, 8, 128), jnp.float32)
                for back in range(8):
                    moved = window if back == 0 else pltpu.roll(window, back, 0)
                    tiles = moved.reshape((ROWS + HALO) // 8, 8, 128)
                    for group in range(taps_len // 8):
                        tap = wide_taps[pass_idx, taps_len - 1 - 8 * group - back, :, cols]
                        start = HALO // 8 - group
                        total = total + tap[None] * tiles[start : start + ROWS // 8]
                depthwise[:, cols] = total.reshape(ROWS, 128)
            hidden = normalise(depthwise[...])
            activated = (hidden * jax.nn.sigmoid(hidden)).astype(jnp.bfloat16)
            mask = row_mask(chunk)
            if chunk == chunks - 1:

                @pl.when(m == 0)
                def _():
                    weight_copies(pass_idx)[1].wait()

            rows = slice(chunk * ROWS, (chunk + 1) * ROWS)
            for block in range(feats // COLS):
                cols = slice(block * COLS, (block + 1) * COLS)
                added = slots[job, rows, cols].astype(jnp.float32) + jnp.dot(
                    activated, w2[pass_idx, :, cols], preferred_element_type=jnp.float32
                )
                outs[job, rows, cols] = jnp.where(mask, added, 0.0).astype(jnp.bfloat16)

            @pl.when(leaving)
            def _():
                for target in range(last):
                    exit_remote(m, chunk, target).start()
                exit_local(m, chunk).start()

            @pl.when(jnp.logical_not(leaving))
            def _():
                slot_copy(job, chunk).start()

        for chunk in reversed(range(chunks)):
            expand(chunk)
            if chunk < chunks - 1:
                finish(chunk + 1)

        @pl.when(tm > 0)
        def _():
            rim_copy(job).wait_recv()
            gated[0:HALO, :] = rims[job].astype(jnp.float32)

        @pl.when(tm == 0)
        def _():
            gated[0:HALO, :] = jnp.zeros((HALO, feats), jnp.float32)

        finish(0)
        return 0

    lax.fori_loop(0, jobs, run_job, 0)


    def drain(job, _):
        leaving = jnp.logical_and(section == last, job >= jobs - micro)

        @pl.when(tm < tms - 1)
        def _():
            rim_copy(job).wait_send()

        for chunk in range(chunks):

            @pl.when(jnp.logical_not(leaving))
            def _():
                slot_copy(job, chunk).wait_send()

        return 0

    lax.fori_loop(0, jobs, drain, 0)

    @pl.when(section == last)
    def _():
        for m in range(micro):
            for chunk in range(chunks):
                for target in range(last):
                    exit_remote(m, chunk, target).wait_send()
                exit_local(m, chunk).wait()

    @pl.when(section != last)
    def _():
        for m in range(micro):
            for chunk in range(chunks):
                exit_remote(m, chunk, 0).wait_recv()


def per_device(inputs, lengths, w_expand, w_project, kernel, gain):
    sections = lax.axis_size("section")
    tms = lax.axis_size("tm")
    micro, frames, width = inputs.shape
    passes, _, feats, expanded = w_expand.shape
    taps = kernel.shape[2]
    chunks = frames // ROWS
    jobs = micro * passes
    hbm = pl.BlockSpec(memory_space=pltpu.HBM)
    dma = pltpu.SemaphoreType.DMA
    return pl.pallas_call(
        functools.partial(relay_kernel, sections, tms),
        out_shape=jax.ShapeDtypeStruct((micro, frames, width), jnp.bfloat16),
        in_specs=[pl.BlockSpec(memory_space=pltpu.SMEM)] + [hbm] * 5,
        out_specs=hbm,
        scratch_shapes=[
            pltpu.VMEM((passes, feats, expanded), jnp.bfloat16),
            pltpu.VMEM((passes, feats, feats), jnp.bfloat16),
            pltpu.VMEM((passes, taps, feats), jnp.float32),
            pltpu.VMEM((passes, 1, feats), jnp.float32),
            pltpu.VMEM((passes, taps, 8, feats), jnp.float32),
            pltpu.VMEM((jobs, frames, feats), jnp.bfloat16),
            pltpu.VMEM((jobs, frames, feats), jnp.bfloat16),
            pltpu.VMEM((jobs, HALO, feats), jnp.bfloat16),
            pltpu.VMEM((jobs, HALO, feats), jnp.bfloat16),
            pltpu.VMEM((HALO + frames, feats), jnp.float32),
            pltpu.VMEM((ROWS, feats), jnp.float32),
            dma((2, passes)),
            dma((2,)),
            dma((jobs, chunks)),
            dma((jobs, chunks)),
            dma((jobs,)),
            dma((jobs,)),
            dma((micro, chunks)),
            dma((micro, chunks, sections)),
            dma((micro, chunks, sections)),
            dma((micro, chunks)),
        ],
        compiler_params=pltpu.CompilerParams(
            collective_id=0, has_side_effects=True, vmem_limit_bytes=63 << 20
        ),
        name="relay",
    )(
        lengths,
        inputs,
        w_expand.reshape(passes, feats, expanded),
        w_project.reshape(passes, feats, feats),
        kernel.reshape(passes, taps, feats),
        gain,
    )


def solution(mesh):
    in_specs = (
        P(None, "tm", "section"),
        P(),
        P(None, "section", None, None),
        P(None, "section", None, None),
        P(None, "section", None, None),
        P(None, "section", None),
    )
    out_specs = P(None, "tm", "section")
    return jax.shard_map(
        per_device, mesh=mesh, in_specs=in_specs, out_specs=out_specs, check_vma=False
    )
```

```python
import functools

import jax
import jax.numpy as jnp
from jax import lax
from jax.experimental import pallas as pl
from jax.experimental.pallas import tpu as pltpu
from jax.sharding import PartitionSpec as P

MESH = pl.DeviceIdType.MESH
ROWS = 32
HALO = 32
COLS = 256
PLAN = (
    ("expand", 3, 2),
    ("finish", 3, 3),
    ("expand", 1, 1),
    ("finish", 2, 2),
    ("expand", 0, 0),
    ("finish", 1, 1),
    ("finish", 0, 0),
)


def normalise(values):
    center = values - jnp.mean(values, axis=-1, keepdims=True)
    variance = jnp.mean(center * center, axis=-1, keepdims=True)
    return center * lax.rsqrt(variance + 1e-05)


def relay_kernel(
    sections,
    tms,
    lengths_ref,
    inputs_hbm,
    w_expand_hbm,
    w_project_hbm,
    kernel_hbm,
    gain_hbm,
    out_hbm,
    w1,
    w2,
    taps,
    gain,
    wide_taps,
    slots,
    outs,
    rims,
    tails,
    gated,
    depthwise,
    w_sems,
    small_sems,
    slot_send,
    slot_recv,
    rim_send,
    rim_recv,
    entry_send,
    entry_recv,
    exit_send,
    exit_recv,
):
    section = lax.axis_index("section")
    tm = lax.axis_index("tm")
    micro, frames, width = inputs_hbm.shape
    passes, feats, _ = w1.shape
    taps_len = taps.shape[1]
    chunks = frames // ROWS
    jobs = micro * passes
    last = sections - 1

    def weight_copies(pass_idx):
        return (
            pltpu.make_async_copy(w_expand_hbm.at[pass_idx], w1.at[pass_idx], w_sems.at[0, pass_idx]),
            pltpu.make_async_copy(w_project_hbm.at[pass_idx], w2.at[pass_idx], w_sems.at[1, pass_idx]),
        )

    taps_copy = pltpu.make_async_copy(kernel_hbm, taps, small_sems.at[0])
    gain_copy = pltpu.make_async_copy(gain_hbm, gain, small_sems.at[1])
    taps_copy.start()
    gain_copy.start()
    for copy in weight_copies(0):
        copy.start()
    for copy in weight_copies(1):
        copy.start()

    barrier = pltpu.get_barrier_semaphore()
    for step in range(1, sections):
        pl.semaphore_signal(
            barrier, inc=1, device_id={"section": (section + step) % sections}, device_id_type=MESH
        )

    @pl.when(tm > 0)
    def _():
        pl.semaphore_signal(barrier, inc=1, device_id={"tm": tm - 1}, device_id_type=MESH)

    @pl.when(tm < tms - 1)
    def _():
        pl.semaphore_signal(barrier, inc=1, device_id={"tm": tm + 1}, device_id_type=MESH)

    greeted = sections - 1 + (tm > 0).astype(jnp.int32) + (tm < tms - 1).astype(jnp.int32)
    pl.semaphore_wait(barrier, greeted)

    def entry_remote(m, chunk, source):
        rows = pl.ds(chunk * ROWS, ROWS)
        return pltpu.make_async_remote_copy(
            src_ref=inputs_hbm.at[m, rows],
            dst_ref=slots.at[m, rows, pl.ds(pl.multiple_of(source * width, width), width)],
            send_sem=entry_send.at[m, chunk],
            recv_sem=entry_recv.at[m, chunk, source],
            device_id={"section": 0},
            device_id_type=MESH,
        )

    def entry_local(m, chunk):
        rows = pl.ds(chunk * ROWS, ROWS)
        return pltpu.make_async_copy(
            inputs_hbm.at[m, rows], slots.at[m, rows, pl.ds(0, width)], entry_recv.at[m, chunk, 0]
        )

    @pl.when(section == 0)
    def _():
        for m in range(micro):
            for chunk in reversed(range(chunks)):
                entry_local(m, chunk).start()

    @pl.when(section != 0)
    def _():
        for m in range(micro):
            for chunk in reversed(range(chunks)):
                entry_remote(m, chunk, section).start()
            for chunk in reversed(range(chunks)):
                entry_remote(m, chunk, section).wait_send()

    taps_copy.wait()
    gain_copy.wait()
    for pass_idx in range(passes):
        for k in range(taps_len):
            wide_taps[pass_idx, k] = jnp.broadcast_to(taps[pass_idx, k : k + 1, :], (8, feats))

    def slot_copy(job, chunk):
        slot = job + jnp.where(section == last, micro, 0)
        rows = pl.ds(pl.multiple_of(chunk * ROWS, ROWS), ROWS)
        return pltpu.make_async_remote_copy(
            src_ref=outs.at[job, rows],
            dst_ref=slots.at[slot, rows],
            send_sem=slot_send.at[job, chunk],
            recv_sem=slot_recv.at[slot, chunk],
            device_id={"section": (section + 1) % sections},
            device_id_type=MESH,
        )

    def slot_arrival(job, chunk):
        rows = pl.ds(pl.multiple_of(chunk * ROWS, ROWS), ROWS)
        return pltpu.make_async_remote_copy(
            src_ref=outs.at[job, rows],
            dst_ref=slots.at[job, rows],
            send_sem=slot_send.at[job, chunk],
            recv_sem=slot_recv.at[job, chunk],
            device_id={"section": (section + 1) % sections},
            device_id_type=MESH,
        )

    def rim_copy(job):
        return pltpu.make_async_remote_copy(
            src_ref=tails.at[job],
            dst_ref=rims.at[job],
            send_sem=rim_send.at[job],
            recv_sem=rim_recv.at[job],
            device_id={"tm": tm + 1},
            device_id_type=MESH,
        )

    def exit_remote(m, chunk, target):
        rows = pl.ds(pl.multiple_of(chunk * ROWS, ROWS), ROWS)
        return pltpu.make_async_remote_copy(
            src_ref=outs.at[m + (jobs - micro), rows, pl.ds(target * width, width)],
            dst_ref=out_hbm.at[m, rows],
            send_sem=exit_send.at[m, chunk, target],
            recv_sem=exit_recv.at[m, chunk],
            device_id={"section": target},
            device_id_type=MESH,
        )

    def exit_local(m, chunk):
        rows = pl.ds(pl.multiple_of(chunk * ROWS, ROWS), ROWS)
        return pltpu.make_async_copy(
            outs.at[m + (jobs - micro), rows, pl.ds(last * width, width)],
            out_hbm.at[m, rows],
            exit_recv.at[m, chunk],
        )

    def run_job(job, _):
        pass_idx = job // micro
        m = job % micro
        length = lengths_ref[m]
        first = jnp.logical_and(section == 0, pass_idx == 0)
        leaving = jnp.logical_and(section == last, pass_idx == passes - 1)

        def row_mask(low, high):
            count = (high + 1 - low) * ROWS
            rows = lax.broadcasted_iota(jnp.int32, (count, 1), 0) + (tm * frames + low * ROWS)
            return rows < length

        def arrive(chunk):
            @pl.when(first)
            def _():
                entry_local(m, chunk).wait()
                for source in range(1, sections):
                    entry_remote(m, chunk, source).wait_recv()

            @pl.when(jnp.logical_not(first))
            def _():
                slot_arrival(job, chunk).wait_recv()

        def expand(high, low):
            for chunk in reversed(range(low, high + 1)):
                arrive(chunk)
            opening = high == chunks - 1
            if opening:

                @pl.when(m == 0)
                def _():
                    weight_copies(pass_idx)[0].wait()

            top, end = low * ROWS, (high + 1) * ROWS
            values = slots[job, top:end, :].astype(jnp.float32)
            normed = (normalise(values) * gain[pass_idx]).astype(jnp.bfloat16)
            mask = row_mask(low, high)
            for block in range(feats // COLS):
                left = block * COLS
                cols = slice(left, left + COLS)
                value = jnp.dot(normed, w1[pass_idx, :, cols], preferred_element_type=jnp.float32)
                gate = jnp.dot(
                    normed,
                    w1[pass_idx, :, feats + left : feats + left + COLS],
                    preferred_element_type=jnp.float32,
                )
                passed = jnp.where(mask, value * jax.nn.sigmoid(gate), 0.0)
                gated[HALO + top : HALO + end, cols] = passed
                if opening:
                    tails[job, :, cols] = passed[end - top - HALO :, :].astype(jnp.bfloat16)
            if opening:

                @pl.when(tm < tms - 1)
                def _():
                    rim_copy(job).start()

        def finish(high, low):
            if low == 0:

                @pl.when(tm > 0)
                def _():
                    rim_copy(job).wait_recv()
                    gated[0:HALO, :] = rims[job].astype(jnp.float32)

                @pl.when(tm == 0)
                def _():
                    gated[0:HALO, :] = jnp.zeros((HALO, feats), jnp.float32)

            top, end = low * ROWS, (high + 1) * ROWS
            count = end - top
            for block in range(feats // 128):
                cols = slice(block * 128, (block + 1) * 128)
                window = gated[top : end + HALO, cols]
                total = jnp.zeros((count // 8, 8, 128), jnp.float32)
                for back in range(8):
                    moved = window if back == 0 else pltpu.roll(window, back, 0)
                    tiles = moved.reshape((count + HALO) // 8, 8, 128)
                    for group in range(taps_len // 8):
                        tap = wide_taps[pass_idx, taps_len - 1 - 8 * group - back, :, cols]
                        start = HALO // 8 - group
                        total = total + tap[None] * tiles[start : start + count // 8]
                depthwise[0:count, cols] = total.reshape(count, 128)
            hidden = normalise(depthwise[0:count, :])
            activated = (hidden * jax.nn.sigmoid(hidden)).astype(jnp.bfloat16)
            mask = row_mask(low, high)
            if high == chunks - 1:

                @pl.when(m == 0)
                def _():
                    weight_copies(pass_idx)[1].wait()

            for block in range(feats // COLS):
                cols = slice(block * COLS, (block + 1) * COLS)
                added = slots[job, top:end, cols].astype(jnp.float32) + jnp.dot(
                    activated, w2[pass_idx, :, cols], preferred_element_type=jnp.float32
                )
                outs[job, top:end, cols] = jnp.where(mask, added, 0.0).astype(jnp.bfloat16)

            @pl.when(leaving)
            def _():
                for chunk in reversed(range(low, high + 1)):
                    for target in range(last):
                        exit_remote(m, chunk, target).start()
                    exit_local(m, chunk).start()

            @pl.when(jnp.logical_not(leaving))
            def _():
                for chunk in reversed(range(low, high + 1)):
                    slot_copy(job, chunk).start()

        for act, high, low in PLAN:
            (expand if act == "expand" else finish)(high, low)
        return 0

    lax.fori_loop(0, jobs, run_job, 0)


    def drain(job, _):
        leaving = jnp.logical_and(section == last, job >= jobs - micro)

        @pl.when(tm < tms - 1)
        def _():
            rim_copy(job).wait_send()

        for chunk in range(chunks):

            @pl.when(jnp.logical_not(leaving))
            def _():
                slot_copy(job, chunk).wait_send()

        return 0

    lax.fori_loop(0, jobs, drain, 0)

    @pl.when(section == last)
    def _():
        for m in range(micro):
            for chunk in range(chunks):
                for target in range(last):
                    exit_remote(m, chunk, target).wait_send()
                exit_local(m, chunk).wait()

    @pl.when(section != last)
    def _():
        for m in range(micro):
            for chunk in range(chunks):
                exit_remote(m, chunk, 0).wait_recv()


def per_device(inputs, lengths, w_expand, w_project, kernel, gain):
    sections = lax.axis_size("section")
    tms = lax.axis_size("tm")
    micro, frames, width = inputs.shape
    passes, _, feats, expanded = w_expand.shape
    taps = kernel.shape[2]
    chunks = frames // ROWS
    jobs = micro * passes
    hbm = pl.BlockSpec(memory_space=pltpu.HBM)
    dma = pltpu.SemaphoreType.DMA
    return pl.pallas_call(
        functools.partial(relay_kernel, sections, tms),
        out_shape=jax.ShapeDtypeStruct((micro, frames, width), jnp.bfloat16),
        in_specs=[pl.BlockSpec(memory_space=pltpu.SMEM)] + [hbm] * 5,
        out_specs=hbm,
        scratch_shapes=[
            pltpu.VMEM((passes, feats, expanded), jnp.bfloat16),
            pltpu.VMEM((passes, feats, feats), jnp.bfloat16),
            pltpu.VMEM((passes, taps, feats), jnp.float32),
            pltpu.VMEM((passes, 1, feats), jnp.float32),
            pltpu.VMEM((passes, taps, 8, feats), jnp.float32),
            pltpu.VMEM((jobs, frames, feats), jnp.bfloat16),
            pltpu.VMEM((jobs, frames, feats), jnp.bfloat16),
            pltpu.VMEM((jobs, HALO, feats), jnp.bfloat16),
            pltpu.VMEM((jobs, HALO, feats), jnp.bfloat16),
            pltpu.VMEM((HALO + frames, feats), jnp.float32),
            pltpu.VMEM((frames, feats), jnp.float32),
            dma((2, passes)),
            dma((2,)),
            dma((jobs, chunks)),
            dma((jobs, chunks)),
            dma((jobs,)),
            dma((jobs,)),
            dma((micro, chunks)),
            dma((micro, chunks, sections)),
            dma((micro, chunks, sections)),
            dma((micro, chunks)),
        ],
        compiler_params=pltpu.CompilerParams(
            collective_id=0, has_side_effects=True, vmem_limit_bytes=63 << 20
        ),
        name="relay",
    )(
        lengths,
        inputs,
        w_expand.reshape(passes, feats, expanded),
        w_project.reshape(passes, feats, feats),
        kernel.reshape(passes, taps, feats),
        gain,
    )


def solution(mesh):
    in_specs = (
        P(None, "tm", "section"),
        P(),
        P(None, "section", None, None),
        P(None, "section", None, None),
        P(None, "section", None, None),
        P(None, "section", None),
    )
    out_specs = P(None, "tm", "section")
    return jax.shard_map(
        per_device, mesh=mesh, in_specs=in_specs, out_specs=out_specs, check_vma=False
    )
```
